32 devices in a mesh: dp: 8 (over z, y), expert: 4 (over x, core).
Axes of the slice: x: 2, y: 2, z: 4, core: 2. Of those that a mesh axis runs over, the one named last changes fastest.
Arguments:
- tokens: bfloat16 [4096, 1024], P(('dp', 'expert')), may hold values from -6 to 6
- route_ids: int32 [4096, 1], P(('dp', 'expert')), may hold values from 0 to 3; in each aligned block of 128 rows (0 to 127, 128 to 255, ...) at most 48 rows name the same one
- route_weight: float32 [4096, 1], P(('dp', 'expert')), may hold values from 0.02 to 0.5
- w_gate_up: bfloat16 [4, 1024, 768], P('expert'), may hold values from -0.1875 to 0.1875
- w_down: bfloat16 [4, 384, 1024], P('expert'), may hold values from -0.3125 to 0.3125
- out_grad: bfloat16 [4096, 1024], P(('dp', 'expert')), may hold values from -6 to 6
Outputs:
- mixed: bfloat16 [4096, 1024], P(('dp', 'expert'))
- token_grad: bfloat16 [4096, 1024], P(('dp', 'expert'))
- route_weight_grad: float32 [4096, 1], P(('dp', 'expert'))
- weight_grad: float32 [4, 1024, 1152], P('expert', 'dp')
The draws below stay inside these ranges and needn't reach their ends.
Inputs may be any that keep to these rules, and one draw needn't show every extreme that they name: `route_ids`: among the 128 rows of one device (aligned blocks), no expert is named by more than 48 rows, a bound that some block reaches; a row names 1 different experts.
All inputs are finite; a program needn't handle non-finite values.
Results may differ from the reference program's by a relative error of at most 0.0057.
Values may be sent and summed in bfloat16 or wider, within the bound.
No kernel may reach another device: no remote copies, remote signals or barrier semaphores. Data moves between devices by JAX's collectives and lax.ppermute only.
A program may use at most 64 MiB of HBM per device.

```python
import math
import jax
import jax.numpy as jnp
import numpy as np
from jax import lax

D = 1024
H = 384
TOK_DEV = 128
TOPK = 1
EXPERTS = 4
CAP = 48
TOKENS = 4096


def shard_levels(stream_key, dims, split, least, high):
    def one(axis_at, parts):
        steps = jax.random.uniform(jax.random.fold_in(jax.random.fold_in(stream_key, 6), axis_at), (parts,), jnp.float32, least / len(split), high / len(split))
        return jnp.repeat(jnp.exp(steps), dims[axis_at] // parts).reshape((-1,) + (1,) * (len(dims) - axis_at - 1))

    gain = one(*split[0])
    for cut in split[1:]:
        gain = gain * one(*cut)
    return gain


def assign_block(own_key, own, number, rows, amount, top, limit, slope):
    sequence = jax.random.permutation(own_key, amount)
    packed, usual = load_shares(amount, rows * top, limit, slope, True), load_shares(amount, rows * top, limit, slope, False)
    places = jnp.arange(amount)

    def named(sizes, turn):
        used = int((sizes > 0).sum())
        fixed = max(1, used // 4)
        shifted = fixed + (places - fixed + turn * (used - fixed)) % max(1, amount - fixed)
        return jnp.zeros((amount,), jnp.int32).at[sequence[jnp.where(places < fixed, places, shifted)]].set(jnp.asarray(sizes, jnp.int32))

    sizes = jnp.where(number % 4 == 0, named(packed, number // 4), named(usual, number - number // 4 - 1))
    mixed = jax.random.permutation(jax.random.fold_in(own, 3), amount)
    giver, sink = mixed[0:amount // 2 * 2:2], mixed[1:amount // 2 * 2:2]
    slack = jnp.minimum(sizes[giver] - 1, limit - sizes[sink]) // 2
    slack = jnp.where((giver == sequence[0]) | (sink == sequence[0]) | (sizes[sink] == 0), 0, jnp.maximum(slack, 0))
    shifted = jax.random.randint(jax.random.fold_in(own, 4), (amount // 2,), 0, 1 << 20) % (slack + 1)
    sizes = sizes.at[giver].add(-shifted).at[sink].add(shifted)
    labels = jnp.searchsorted(jnp.cumsum(sizes), jnp.arange(rows * top), side="right").astype(jnp.int32)
    table = labels.reshape(top, rows).T
    table = table[jax.random.permutation(jax.random.fold_in(own, 1), rows)]
    turn = jax.random.randint(jax.random.fold_in(own, 2), (rows, 1), 0, top)
    return jnp.take_along_axis(table, (jnp.arange(top)[None, :] + turn) % top, axis=1)


def load_shares(count, total, limit, lean, full):
    loads = [(1 << 20) // math.isqrt(standing ** lean) + 1 for standing in range(1, count + 1)]
    largest = limit if full else min(limit, max(-(-total // count), total * loads[0] // sum(loads)))
    least = 1 if total - largest >= count - 1 else 0
    given, rest = [largest] + [least] * (count - 1), total - largest - least * (count - 1)
    while rest > 0:
        movable = [i for i in range(1, count) if given[i] < largest] or [i for i in range(1, count) if given[i] < limit]
        mass, budget = sum([loads[i] for i in movable]), rest
        for i in movable:
            extra = min(limit - given[i], max(1, budget * loads[i] // mass), rest)
            given[i] = given[i] + extra
            rest = rest - extra
    return np.array(given)


def scatter_about(own_key, extent, scale, most, split=(), kind=jnp.bfloat16):
    loudness = shard_levels(own_key, extent, split, -0.22, 0.18) if split else 1.0
    values = jax.random.normal(own_key, extent, jnp.float32) * scale * loudness
    return jnp.minimum(jnp.maximum(values, -most), most).astype(kind)


def setup_inputs(seed: int = 0) -> dict:
    key_of = jax.random.split(jax.random.key(seed), 7)
    tokens = scatter_about(key_of[0], (TOKENS, D), 1.0, 6.0, ((0, 32),))
    route_ids_keys = jax.random.split(jax.random.fold_in(key_of[1], 1), TOKENS // TOK_DEV)
    route_ids_turns = jax.random.permutation(jax.random.fold_in(key_of[1], 3), TOKENS // TOK_DEV)
    route_ids = jax.vmap(lambda own, number: assign_block(jax.random.fold_in(key_of[1], 2), own, number, TOK_DEV, EXPERTS, TOPK, CAP, 2))(route_ids_keys, route_ids_turns).reshape((TOKENS, TOPK))
    route_weight = jnp.clip(jnp.exp(math.log(0.5) - 3.218876 * jax.random.uniform(key_of[2], (TOKENS, TOPK), jnp.float32) ** shard_levels(key_of[2], (TOKENS, TOPK), ((0, 32),), -0.2, 0.2)), 0.02, 0.5)
    w_gate_up = scatter_about(key_of[3], (EXPERTS, D, 2 * H), D ** -0.5, 0.1875, ((0, 4),))
    w_down = scatter_about(key_of[4], (EXPERTS, H, D), H ** -0.5, 0.3125, ((0, 4),))
    out_grad = scatter_about(key_of[5], (TOKENS, D), 1.0, 6.0, ((0, 32),))
    return dict(tokens=tokens, route_ids=route_ids, route_weight=route_weight, w_gate_up=w_gate_up, w_down=w_down, out_grad=out_grad)


def reference(tokens, route_ids, route_weight, w_gate_up, w_down, out_grad):
    count = tokens.shape[0]
    width = tokens.shape[1]
    hidden = w_down.shape[1]
    blocks = count // TOK_DEV
    per_block = TOK_DEV * TOPK
    ids = route_ids.reshape(blocks, per_block)
    onehot = (ids[:, :, None] == jnp.arange(EXPERTS, dtype=jnp.int32)[None, None, :]).astype(jnp.int32)
    position = jnp.sum((jnp.cumsum(onehot, axis=1) - onehot) * onehot, axis=2).astype(jnp.int32)
    copy_index = (jnp.arange(blocks, dtype=jnp.int32)[:, None] * per_block
                  + jnp.arange(per_block, dtype=jnp.int32)[None, :]).astype(jnp.int32)
    table = jnp.full((EXPERTS, blocks, CAP), count * TOPK, jnp.int32)
    block_rows = jnp.broadcast_to(jnp.arange(blocks, dtype=jnp.int32)[:, None], (blocks, per_block))
    table = table.at[ids, block_rows, position].set(copy_index)
    token_pad = jnp.concatenate([tokens, jnp.zeros((1, width), tokens.dtype)], axis=0)
    grad_pad = jnp.concatenate([out_grad, jnp.zeros((1, width), out_grad.dtype)], axis=0)
    weight_pad = jnp.concatenate([route_weight.reshape(-1), jnp.zeros((1,), jnp.float32)], axis=0)

    def per_expert(carry, inputs):
        mixed_sum, dx_sum, route_sum = carry
        slots, gate_up, down = inputs
        flat = slots.reshape(-1)
        source = (flat // TOPK).astype(jnp.int32)
        rows = token_pad[source]
        pre = jnp.dot(rows, gate_up, preferred_element_type=jnp.float32)
        gate_pre = pre[:, :hidden]
        up_pre = pre[:, hidden:]
        sig = jax.nn.sigmoid(gate_pre)
        silu_gate = gate_pre * sig
        act = (silu_gate * up_pre).astype(jnp.bfloat16)
        result = jnp.dot(act, down, preferred_element_type=jnp.float32).astype(jnp.bfloat16)
        result_f = result.astype(jnp.float32)
        scale = weight_pad[flat]
        mixed_sum = mixed_sum.at[source].add(scale[:, None] * result_f)
        upstream = grad_pad[source].astype(jnp.float32)
        route_sum = route_sum.at[flat].add(jnp.sum(upstream * result_f, axis=1))
        cotan = (scale[:, None] * upstream).astype(jnp.bfloat16)
        d_act = jnp.dot(cotan, down.T, preferred_element_type=jnp.float32)
        d_gate = d_act * up_pre * sig * (1.0 + gate_pre * (1.0 - sig))
        d_up = d_act * silu_gate
        d_pre = jnp.concatenate([d_gate, d_up], axis=1).astype(jnp.bfloat16)
        dx_rows = jnp.dot(d_pre, gate_up.T, preferred_element_type=jnp.float32).astype(jnp.bfloat16)
        dx_sum = dx_sum.at[source].add(dx_rows.astype(jnp.float32))
        grad_gu = jnp.dot(rows.T, d_pre, preferred_element_type=jnp.float32)
        grad_down = jnp.dot(cotan.T, act, preferred_element_type=jnp.float32)
        return (mixed_sum, dx_sum, route_sum), jnp.concatenate([grad_gu, grad_down], axis=1)

    init = (jnp.zeros((count + 1, width), jnp.float32), jnp.zeros((count + 1, width), jnp.float32),
            jnp.zeros((count * TOPK + 1,), jnp.float32))
    final, grads = lax.scan(per_expert, init, (table, w_gate_up, w_down))
    mixed_sum, dx_sum, route_sum = final
    return (mixed_sum[:count].astype(jnp.bfloat16), dx_sum[:count].astype(jnp.bfloat16),
            route_sum[:count * TOPK].reshape(count, TOPK), grads)
```

```python
import functools

import jax
import jax.numpy as jnp
from jax import lax
from jax.experimental import pallas as pl
from jax.experimental.pallas import tpu as pltpu
from jax.sharding import PartitionSpec as P

BF = jnp.bfloat16
F32 = jnp.float32
VMEM = pl.BlockSpec(memory_space=pltpu.VMEM)


def dot(left, right, left_axis, right_axis):
    return lax.dot_general(
        left, right, (((left_axis,), (right_axis,)), ((), ())), preferred_element_type=F32
    )


def call(body, name, outs, args, scratch=(), flops=0):
    size = sum(a.size * a.dtype.itemsize for a in args)
    size += sum(o.size * o.dtype.itemsize for o in outs)
    return pl.pallas_call(
        body,
        name=name,
        out_shape=list(outs),
        in_specs=[VMEM] * len(args),
        out_specs=[VMEM] * len(outs),
        scratch_shapes=list(scratch),
        cost_estimate=pl.CostEstimate(flops=flops, bytes_accessed=size, transcendentals=0),
        compiler_params=pltpu.CompilerParams(vmem_limit_bytes=24 << 20),
    )(*args)


def shape(dims, dtype):
    return jax.ShapeDtypeStruct(dims, dtype)


def row_to_column(row):
    count = row.shape[1]
    at = lax.broadcasted_iota(jnp.int32, (count, count), 0)
    to = lax.broadcasted_iota(jnp.int32, (count, count), 1)
    return jnp.sum(jnp.where(at == to, jnp.broadcast_to(row, (count, count)), 0.0), axis=1, keepdims=True)


def column_to_row(column):
    count = column.shape[0]
    at = lax.broadcasted_iota(jnp.int32, (count, count), 0)
    to = lax.broadcasted_iota(jnp.int32, (count, count), 1)
    return jnp.sum(jnp.where(at == to, jnp.broadcast_to(column, (count, count)), 0.0), axis=0, keepdims=True)


def dispatch_body(experts, slots, ids, weight, tokens, out_grad, placed_out, *blocks):
    me = lax.axis_index("expert")
    count = ids.shape[1]
    padded = max(8, experts)
    kinds = lax.broadcasted_iota(jnp.int32, (padded, count), 0)
    here = kinds == jnp.broadcast_to(ids[...], (padded, count))
    onehot = jnp.where(here, 1.0, 0.0)
    at = lax.broadcasted_iota(jnp.int32, (count, count), 0)
    to = lax.broadcasted_iota(jnp.int32, (count, count), 1)
    earlier = jnp.where(at < to, 1.0, 0.0).astype(BF)
    before = dot(onehot.astype(BF), earlier, 1, 0)
    position = jnp.sum(before * onehot, axis=0, keepdims=True).astype(jnp.int32)
    slot = (ids[...] ^ me) * slots + position
    rows = experts * slots
    place = lax.broadcasted_iota(jnp.int32, (rows, count), 0)
    placed = jnp.where(place == jnp.broadcast_to(slot, (rows, count)), 1.0, 0.0).astype(BF)
    placed_out[...] = placed
    sent = dot(placed, tokens[...], 1, 0).astype(BF)
    for k in range(experts):
        blocks[k][...] = sent[k * slots:(k + 1) * slots]
    scaled = (row_to_column(weight[...]) * out_grad[...].astype(F32)).astype(BF)
    sent = dot(placed, scaled, 1, 0).astype(BF)
    for k in range(experts):
        blocks[experts + k][...] = sent[k * slots:(k + 1) * slots]


def split_columns(rows, own, other, parts, width):
    side = lax.rem(lax.axis_index("dp"), 2)
    for k in range(parts):
        mine = pl.multiple_of((2 * k + side) * width, width)
        theirs = pl.multiple_of((2 * k + 1 - side) * width, width)
        own[:, k * width:(k + 1) * width] = rows[:, pl.ds(mine, width)]
        other[:, k * width:(k + 1) * width] = rows[:, pl.ds(theirs, width)]


def forward_body(experts, parts, width, *refs):
    blocks, (gate_up, pre_out, own, send, rows) = refs[:experts], refs[experts:]
    slots = blocks[0].shape[0]
    for k in range(experts):
        rows[k * slots:(k + 1) * slots, :] = blocks[k][...]
    pre = dot(rows[...], gate_up[0], 1, 0)
    pre_out[...] = pre
    hidden = pre.shape[1] // 2
    gate, up = pre[:, :hidden], pre[:, hidden:]
    act = (gate * jax.nn.sigmoid(gate) * up).astype(BF)
    half = parts * width
    send[:, half:] = act
    split_columns(rows, own, send, parts, width)


def backward_body(experts, parts, width, *refs):
    blocks, (pre, down, own, send, rows) = refs[:experts], refs[experts:]
    slots = blocks[0].shape[0]
    for k in range(experts):
        rows[k * slots:(k + 1) * slots, :] = blocks[k][...]
    d_act = dot(rows[...], down[0], 1, 1)
    hidden = d_act.shape[1]
    gate, up = pre[:, :hidden], pre[:, hidden:]
    sig = jax.nn.sigmoid(gate)
    half = parts * width
    send[:, half:half + hidden] = (d_act * up * sig * (1.0 + gate * (1.0 - sig))).astype(BF)
    send[:, half + hidden:] = (d_act * (gate * sig)).astype(BF)
    split_columns(rows, own, send, parts, width)


def return_body(experts, half, first, second, gate_up, down, *blocks):
    slots = blocks[0].shape[0]
    result = dot(first[:, half:], down[0], 1, 0).astype(BF)
    for k in range(experts):
        blocks[k][...] = result[k * slots:(k + 1) * slots]
    moved = dot(second[:, half:], gate_up[0], 1, 1).astype(BF)
    for k in range(experts):
        blocks[experts + k][...] = moved[k * slots:(k + 1) * slots]


def weight_body(parts, width, rows, grads, first, second, first_in, second_in, kept, *blocks):
    half = parts * width
    place = lax.axis_index("dp") // 2
    hidden = first.shape[1] - half
    for k in range(parts):
        at = pl.multiple_of((place ^ k) * width, width)
        gate_up = dot(rows[:, pl.ds(at, width)], second[:, half:], 0, 0)
        gate_up += dot(first_in[:, pl.ds(at, width)], second_in[:, half:], 0, 0)
        down = dot(grads[:, pl.ds(at, width)], first[:, half:], 0, 0)
        down += dot(second_in[:, pl.ds(at, width)], first_in[:, half:], 0, 0)
        out = kept if k == 0 else blocks[k - 1]
        out[:, :2 * hidden] = gate_up.astype(out.dtype)
        out[:, 2 * hidden:] = down.astype(out.dtype)


def combine_body(experts, *refs):
    results, moved = refs[:experts], refs[experts:2 * experts]
    placed, weight, out_grad, mixed, token_grad, weight_out, rows = refs[2 * experts:]
    slots = results[0].shape[0]
    for k in range(experts):
        rows[k * slots:(k + 1) * slots, :] = results[k][...]
    copy_out = dot(placed[...], rows[...], 0, 0)
    mixed[...] = (row_to_column(weight[...]) * copy_out).astype(BF)
    products = jnp.sum(out_grad[...].astype(F32) * copy_out, axis=1, keepdims=True)
    weight_out[...] = column_to_row(products)
    for k in range(experts):
        rows[k * slots:(k + 1) * slots, :] = moved[k][...]
    token_grad[...] = dot(placed[...], rows[...], 0, 0).astype(BF)


def exchange(blocks, axis, size, stride=1):
    out = [blocks[0]]
    for k in range(1, len(blocks)):
        out.append(lax.ppermute(blocks[k], axis, [(i, i ^ (k * stride)) for i in range(size)]))
    return out


def on_device(tokens, route_ids, route_weight, w_gate_up, w_down, out_grad):
    experts, shards = lax.axis_size("expert"), lax.axis_size("dp")
    count, top = route_ids.shape
    assert top == 1
    width = tokens.shape[1]
    hidden = w_down.shape[1]
    capacity = 3 * count // (2 * experts)
    slots = -(-capacity // 16) * 16
    rows = experts * slots
    share = width // shards
    staged = shards % 2 == 0 and share % 128 == 0
    parts, piece = (shards // 2, share) if staged else (width // 256, 128)
    half = parts * piece
    ids = route_ids.reshape(1, count)
    weight = route_weight.reshape(1, count)

    block = shape((slots, width), BF)
    placed, *sent = call(
        functools.partial(dispatch_body, experts, slots), "dispatch",
        [shape((rows, count), BF)] + [block] * (2 * experts),
        (ids, weight, tokens, out_grad), flops=4 * rows * count * width)
    token_blocks = exchange(sent[:experts], "expert", experts)
    grad_blocks = exchange(sent[experts:], "expert", experts)
    scratch = [pltpu.VMEM((rows, width), BF)]
    pre, own_rows, first = call(
        functools.partial(forward_body, experts, parts, piece), "forward",
        [shape((rows, 2 * hidden), F32), shape((rows, half), BF), shape((rows, half + hidden), BF)],
        (*token_blocks, w_gate_up), scratch, flops=4 * rows * hidden * width)
    own_grads, second = call(
        functools.partial(backward_body, experts, parts, piece), "backward",
        [shape((rows, half), BF), shape((rows, half + 2 * hidden), BF)],
        (*grad_blocks, pre, w_down), scratch, flops=2 * rows * hidden * width)
    back = call(
        functools.partial(return_body, experts, half), "returns", [block] * (2 * experts),
        (first, second, w_gate_up, w_down), flops=6 * rows * hidden * width)
    if staged:
        pairs = [(i, i ^ 1) for i in range(shards)]
        first_in = lax.ppermute(first, "dp", pairs)
        second_in = lax.ppermute(second, "dp", pairs)
        kept, *partial = call(
            functools.partial(weight_body, parts, piece), "weights",
            [shape((share, 3 * hidden), F32)] + [shape((share, 3 * hidden), BF)] * (parts - 1),
            (own_rows, own_grads, first, second, first_in, second_in),
            flops=12 * rows * hidden * half)
        arrived = exchange([kept] + partial, "dp", shards, 2)
        weight_grad = arrived[0]
        for term in arrived[1:]:
            weight_grad = weight_grad + term.astype(F32)
    else:
        weight_grad = lax.psum_scatter(
            jnp.concatenate([
                dot(jnp.concatenate(token_blocks, axis=0), second[:, half:], 0, 0),
                dot(jnp.concatenate(grad_blocks, axis=0), first[:, half:], 0, 0)], axis=1),
            "dp", scatter_dimension=0, tiled=True)
    results = exchange(back[:experts], "expert", experts)
    moved = exchange(back[experts:], "expert", experts)
    mixed, token_grad, weight_row = call(
        functools.partial(combine_body, experts), "combine",
        [shape((count, width), BF), shape((count, width), BF), shape((1, count), F32)],
        (*results, *moved, placed, weight, out_grad), scratch, flops=4 * rows * count * width)
    return (mixed, token_grad, weight_row.reshape(count, 1), weight_grad[None])


def solution(mesh):
    split = P(("dp", "expert"), None)
    whole = P("expert", None, None)
    return jax.shard_map(
        on_device,
        mesh=mesh,
        in_specs=(split, split, split, whole, whole, split),
        out_specs=(split, split, split, P("expert", "dp", None)),
        check_vma=False,
    )
```

```python
import functools

import jax
import jax.numpy as jnp
from jax import lax
from jax.experimental import pallas as pl
from jax.experimental.pallas import tpu as pltpu
from jax.sharding import PartitionSpec as P


BF = jnp.bfloat16
F32 = jnp.float32
VMEM = pl.BlockSpec(memory_space=pltpu.VMEM)
ANY = pl.BlockSpec(memory_space=pltpu.HBM)


def dot(left, right, left_axis, right_axis):
    return lax.dot_general(
        left, right, (((left_axis,), (right_axis,)), ((), ())), preferred_element_type=F32
    )


def call(body, outs, args, scratch=(), flops=0, spec=VMEM):
    size = sum(a.size * a.dtype.itemsize for a in args)
    size += sum(o.size * o.dtype.itemsize for o in outs)
    return pl.pallas_call(
        body,
        out_shape=list(outs),
        in_specs=[spec] * len(args),
        out_specs=[VMEM] * len(outs),
        scratch_shapes=list(scratch),
        cost_estimate=pl.CostEstimate(flops=flops, bytes_accessed=size, transcendentals=0),
        compiler_params=pltpu.CompilerParams(vmem_limit_bytes=24 << 20),
    )(*args)


def shape(dims, dtype):
    return jax.ShapeDtypeStruct(dims, dtype)


def row_to_column(row):
    count = row.shape[1]
    at = lax.broadcasted_iota(jnp.int32, (count, count), 0)
    to = lax.broadcasted_iota(jnp.int32, (count, count), 1)
    return jnp.sum(jnp.where(at == to, jnp.broadcast_to(row, (count, count)), 0.0), axis=1, keepdims=True)


def column_to_row(column):
    count = column.shape[0]
    at = lax.broadcasted_iota(jnp.int32, (count, count), 0)
    to = lax.broadcasted_iota(jnp.int32, (count, count), 1)
    return jnp.sum(jnp.where(at == to, jnp.broadcast_to(column, (count, count)), 0.0), axis=0, keepdims=True)


def dispatch_body(experts, slots, parts, width, *refs):
    placed_out, gate_up_out, down_out, *blocks = refs[6:-5]
    held, sems = refs[-5:-1], refs[-1]
    landing = (*held, gate_up_out, down_out)
    copies = [pltpu.make_async_copy(refs[k], landing[k], sems.at[k]) for k in range(6)]
    for copy in copies:
        copy.start()
    ids, weight, tokens, out_grad = held
    me = lax.axis_index("expert")
    side = lax.rem(lax.axis_index("dp"), 2)
    count = ids.shape[1]
    padded = max(8, experts)
    copies[0].wait()
    kinds = lax.broadcasted_iota(jnp.int32, (padded, count), 0)
    here = kinds == jnp.broadcast_to(ids[...], (padded, count))
    onehot = jnp.where(here, 1.0, 0.0)
    at = lax.broadcasted_iota(jnp.int32, (count, count), 0)
    to = lax.broadcasted_iota(jnp.int32, (count, count), 1)
    earlier = jnp.where(at < to, 1.0, 0.0).astype(BF)
    before = dot(onehot.astype(BF), earlier, 1, 0)
    position = jnp.sum(before * onehot, axis=0, keepdims=True).astype(jnp.int32)
    slot = (ids[...] ^ me) * slots + position
    rows = experts * slots
    place = lax.broadcasted_iota(jnp.int32, (rows, count), 0)
    placed = jnp.where(place == jnp.broadcast_to(slot, (rows, count)), 1.0, 0.0).astype(BF)
    placed_out[...] = placed
    copies[2].wait()
    sent = dot(placed, tokens[...], 1, 0).astype(BF)
    for k in range(experts):
        blocks[k][...] = sent[k * slots:(k + 1) * slots]
    copies[1].wait()
    copies[3].wait()
    scaled = (row_to_column(weight[...]) * out_grad[...].astype(F32)).astype(BF)
    sent = dot(placed, scaled, 1, 0).astype(BF)
    for k in range(experts):
        blocks[experts + k][...] = sent[k * slots:(k + 1) * slots]
    for k in range(len(blocks) - 2 * experts):
        half = blocks[2 * experts + k]
        for m in range(parts):
            theirs = pl.multiple_of((2 * m + 1 - side) * width, width)
            half[:, m * width:(m + 1) * width] = blocks[k][:, pl.ds(theirs, width)]
            half[:, (parts + m) * width:(parts + m + 1) * width] = blocks[experts + k][:, pl.ds(theirs, width)]
    copies[4].wait()
    copies[5].wait()


def own_columns(rows, own, parts, width):
    side = lax.rem(lax.axis_index("dp"), 2)
    for k in range(parts):
        mine = pl.multiple_of((2 * k + side) * width, width)
        own[:, k * width:(k + 1) * width] = rows[:, pl.ds(mine, width)]


def forward_body(experts, parts, width, *refs):
    blocks, (gate_up, pre_out, own, act_out, rows) = refs[:experts], refs[experts:]
    slots = blocks[0].shape[0]
    for k in range(experts):
        rows[k * slots:(k + 1) * slots, :] = blocks[k][...]
    pre = dot(rows[...], gate_up[0], 1, 0)
    pre_out[...] = pre
    hidden = pre.shape[1] // 2
    gate, up = pre[:, :hidden], pre[:, hidden:]
    act_out[...] = (gate * jax.nn.sigmoid(gate) * up).astype(BF)
    own_columns(rows, own, parts, width)


def backward_body(experts, parts, width, *refs):
    blocks, (pre, down, own, d_pre, rows) = refs[:experts], refs[experts:]
    slots = blocks[0].shape[0]
    for k in range(experts):
        rows[k * slots:(k + 1) * slots, :] = blocks[k][...]
    d_act = dot(rows[...], down[0], 1, 1)
    hidden = d_act.shape[1]
    gate, up = pre[:, :hidden], pre[:, hidden:]
    sig = jax.nn.sigmoid(gate)
    d_pre[:, :hidden] = (d_act * up * sig * (1.0 + gate * (1.0 - sig))).astype(BF)
    d_pre[:, hidden:] = (d_act * (gate * sig)).astype(BF)
    own_columns(rows, own, parts, width)


def return_body(experts, act, d_pre, gate_up, down, *blocks):
    slots = blocks[0].shape[0] // 2
    result = dot(act[...], down[0], 1, 0).astype(BF)
    for k in range(experts):
        blocks[k][:slots] = result[k * slots:(k + 1) * slots]
    moved = dot(d_pre[...], gate_up[0], 1, 1).astype(BF)
    for k in range(experts):
        blocks[k][slots:] = moved[k * slots:(k + 1) * slots]


def weight_body(experts, parts, width, offset, *refs):
    halves, (own, factor, factor_in, *outs, rows) = refs[:experts], refs[experts:]
    slots = halves[0].shape[0]
    for k in range(experts):
        rows[k * slots:(k + 1) * slots, :] = halves[k][:, offset:offset + parts * width]
    place = lax.axis_index("dp") // 2
    for k in range(parts):
        at = pl.multiple_of((place ^ k) * width, width)
        total = dot(own[:, pl.ds(at, width)], factor[...], 0, 0)
        total += dot(rows[:, pl.ds(at, width)], factor_in[...], 0, 0)
        outs[k][...] = total.astype(outs[k].dtype)


def sum_body(parts, *refs):
    first, second, out = refs[:parts], refs[parts:2 * parts], refs[2 * parts]
    cut = first[0].shape[1]
    total = first[0][...]
    for k in range(1, parts):
        total += first[k][...].astype(F32)
    out[:, :cut] = total
    total = second[0][...]
    for k in range(1, parts):
        total += second[k][...].astype(F32)
    out[:, cut:] = total


def combine_body(experts, *refs):
    blocks = refs[:experts]
    placed, weight, out_grad, mixed, token_grad, weight_out, rows = refs[experts:]
    slots = blocks[0].shape[0] // 2
    for k in range(experts):
        rows[k * slots:(k + 1) * slots, :] = blocks[k][:slots]
    copy_out = dot(placed[...], rows[...], 0, 0)
    mixed[...] = (row_to_column(weight[...]) * copy_out).astype(BF)
    products = jnp.sum(out_grad[...].astype(F32) * copy_out, axis=1, keepdims=True)
    weight_out[...] = column_to_row(products)
    for k in range(experts):
        rows[k * slots:(k + 1) * slots, :] = blocks[k][slots:]
    token_grad[...] = dot(placed[...], rows[...], 0, 0).astype(BF)


def far(*arrays):
    return [pltpu.with_memory_space_constraint(a, pltpu.HBM) for a in arrays]


def exchange(blocks, axis, size, stride=1):
    out = [blocks[0]]
    for k in range(1, len(blocks)):
        out.append(lax.ppermute(blocks[k], axis, [(i, i ^ (k * stride)) for i in range(size)]))
    return out


def across(blocks, experts, shards):
    out = []
    for k in range(experts):
        pairs = [
            (i * experts + j, (i ^ 1) * experts + (j ^ k))
            for i in range(shards) for j in range(experts)
        ]
        out.append(lax.ppermute(blocks[k], ("dp", "expert"), pairs))
    return out


def on_device(tokens, route_ids, route_weight, w_gate_up, w_down, out_grad):
    experts, shards = lax.axis_size("expert"), lax.axis_size("dp")
    count, top = route_ids.shape
    assert top == 1
    width = tokens.shape[1]
    hidden = w_down.shape[1]
    capacity = 3 * count // (2 * experts)
    slots = -(-capacity // 16) * 16
    rows = experts * slots
    share = width // shards
    staged = is_staged(width, shards)
    parts, piece = (shards // 2, share) if staged else (width // 256, 128)
    half = parts * piece
    ids = route_ids.reshape(1, count)
    weight = route_weight.reshape(1, count)

    block = shape((slots, width), BF)
    placed, gate_up, down, *sent = call(
        functools.partial(dispatch_body, experts, slots, parts, piece),
        [shape((rows, count), BF), shape(w_gate_up.shape, BF), shape(w_down.shape, BF)]
        + [block] * ((3 if staged else 2) * experts),
        far(ids, weight, tokens, out_grad, w_gate_up, w_down),
        [pltpu.VMEM(a.shape, a.dtype) for a in (ids, weight, tokens, out_grad)]
        + [pltpu.SemaphoreType.DMA((6,))],
        flops=4 * rows * count * width, spec=ANY)
    token_blocks = exchange(sent[:experts], "expert", experts)
    grad_blocks = exchange(sent[experts:2 * experts], "expert", experts)
    scratch = [pltpu.VMEM((rows, width), BF)]
    pre, own_rows, act = call(
        functools.partial(forward_body, experts, parts, piece),
        [shape((rows, 2 * hidden), F32), shape((rows, half), BF), shape((rows, hidden), BF)],
        (*token_blocks, gate_up), scratch, flops=4 * rows * hidden * width)
    own_grads, d_pre = call(
        functools.partial(backward_body, experts, parts, piece),
        [shape((rows, half), BF), shape((rows, 2 * hidden), BF)],
        (*grad_blocks, pre, down), scratch, flops=2 * rows * hidden * width)
    back = call(
        functools.partial(return_body, experts), [shape((2 * slots, width), BF)] * experts,
        (act, d_pre, gate_up, down), flops=6 * rows * hidden * width)
    if staged:
        act_in = exchange([act, act], "dp", shards)[1]
        halves = across(sent[2 * experts:], experts, shards)
        d_pre_in = exchange([d_pre, d_pre], "dp", shards)[1]
        scratch_half = [pltpu.VMEM((rows, half), BF)]
        downs = call(
            functools.partial(weight_body, experts, parts, piece, half),
            [shape((share, hidden), F32)] + [shape((share, hidden), BF)] * (parts - 1),
            (*halves, own_grads, act, act_in), scratch_half, flops=4 * rows * hidden * half)
        downs = exchange(downs, "dp", shards, 2)
        ups = call(
            functools.partial(weight_body, experts, parts, piece, 0),
            [shape((share, 2 * hidden), F32)] + [shape((share, 2 * hidden), BF)] * (parts - 1),
            (*halves, own_rows, d_pre, d_pre_in), scratch_half, flops=8 * rows * hidden * half)
        ups = exchange(ups, "dp", shards, 2)
        weight_grad, = call(
            functools.partial(sum_body, parts), [shape((share, 3 * hidden), F32)],
            (*ups, *downs))
    else:
        weight_grad = lax.psum_scatter(
            jnp.concatenate([
                dot(jnp.concatenate(token_blocks, axis=0), d_pre, 0, 0),
                dot(jnp.concatenate(grad_blocks, axis=0), act, 0, 0)], axis=1),
            "dp", scatter_dimension=0, tiled=True)
    returned = exchange(back, "expert", experts)
    mixed, token_grad, weight_row = call(
        functools.partial(combine_body, experts),
        [shape((count, width), BF), shape((count, width), BF), shape((1, count), F32)],
        (*returned, placed, weight, out_grad), scratch, flops=4 * rows * count * width)
    return (mixed, token_grad, weight_row.reshape(count, 1), weight_grad[None])


def is_staged(width, shards):
    return shards % 2 == 0 and (width // shards) % 128 == 0


def solution(mesh):
    split = P(("dp", "expert"), None)
    whole = P("expert", None, None)

    return jax.shard_map(
        on_device,
        mesh=mesh,
        in_specs=(split, split, split, whole, whole, split),
        out_specs=(split, split, split, P("expert", "dp", None)),
        check_vma=False,
    )
```

```python
import functools

import jax
import jax.numpy as jnp
from jax import lax
from jax.experimental import pallas as pl
from jax.experimental.pallas import tpu as pltpu
from jax.sharding import PartitionSpec as P


BF = jnp.bfloat16
F32 = jnp.float32
VMEM = pl.BlockSpec(memory_space=pltpu.VMEM)
FAR = pl.BlockSpec(memory_space=pltpu.HBM)


def dot(left, right, left_axis, right_axis):
    return lax.dot_general(
        left, right, (((left_axis,), (right_axis,)), ((), ())), preferred_element_type=F32
    )


def call(body, outs, args, scratch=(), flops=0, far_ins=(), far_outs=(), aliases=None):
    size = sum(a.size * a.dtype.itemsize for a in args)
    size += sum(o.size * o.dtype.itemsize for o in outs)
    args = [pltpu.with_memory_space_constraint(a, pltpu.HBM) if k in far_ins else a for k, a in enumerate(args)]
    return pl.pallas_call(
        body,
        out_shape=list(outs),
        in_specs=[FAR if k in far_ins else VMEM for k in range(len(args))],
        out_specs=[FAR if k in far_outs else VMEM for k in range(len(outs))],
        scratch_shapes=list(scratch),
        input_output_aliases=aliases or {},
        cost_estimate=pl.CostEstimate(flops=flops, bytes_accessed=size, transcendentals=0),
        compiler_params=pltpu.CompilerParams(vmem_limit_bytes=24 << 20),
    )(*args)


def shape(dims, dtype):
    return jax.ShapeDtypeStruct(dims, dtype)


def row_to_column(row):
    count = row.shape[1]
    at = lax.broadcasted_iota(jnp.int32, (count, count), 0)
    to = lax.broadcasted_iota(jnp.int32, (count, count), 1)
    return jnp.sum(jnp.where(at == to, jnp.broadcast_to(row, (count, count)), 0.0), axis=1, keepdims=True)


def column_to_row(column):
    count = column.shape[0]
    at = lax.broadcasted_iota(jnp.int32, (count, count), 0)
    to = lax.broadcasted_iota(jnp.int32, (count, count), 1)
    return jnp.sum(jnp.where(at == to, jnp.broadcast_to(column, (count, count)), 0.0), axis=0, keepdims=True)


def one_hot(ids, experts, slots):
    me = lax.axis_index("expert")
    count = ids.shape[1]
    padded = max(8, experts)
    kinds = lax.broadcasted_iota(jnp.int32, (padded, count), 0)
    here = kinds == jnp.broadcast_to(ids, (padded, count))
    onehot = jnp.where(here, 1.0, 0.0)
    at = lax.broadcasted_iota(jnp.int32, (count, count), 0)
    to = lax.broadcasted_iota(jnp.int32, (count, count), 1)
    earlier = jnp.where(at < to, 1.0, 0.0).astype(BF)
    before = dot(onehot.astype(BF), earlier, 1, 0)
    position = jnp.sum(before * onehot, axis=0, keepdims=True).astype(jnp.int32)
    slot = (ids ^ me) * slots + position
    rows = experts * slots
    place = lax.broadcasted_iota(jnp.int32, (rows, count), 0)
    return jnp.where(place == jnp.broadcast_to(slot, (rows, count)), 1.0, 0.0).astype(BF)


def copy_in(sources, targets, sems):
    copies = [pltpu.make_async_copy(s, t, sems.at[k]) for k, (s, t) in enumerate(zip(sources, targets))]
    for copy in copies:
        copy.start()
    return copies


def tokens_body(experts, slots, ids_in, tokens_in, placed_out, *refs):
    blocks, (ids, tokens, sems) = refs[:experts], refs[experts:]
    copies = copy_in((ids_in, tokens_in), (ids, tokens), sems)
    copies[0].wait()
    placed = one_hot(ids[...], experts, slots)
    placed_out[...] = placed
    copies[1].wait()
    sent = dot(placed, tokens[...], 1, 0).astype(BF)
    for k in range(experts):
        blocks[k][...] = sent[k * slots:(k + 1) * slots]


def grads_body(experts, width, *refs):
    placed, *token_blocks = refs[:experts + 1]
    sources = refs[experts + 1:experts + 5]
    gate_up, down, *blocks = refs[experts + 5:-3]
    weight, out_grad, sems = refs[-3:]
    copies = copy_in(sources, (weight, out_grad, gate_up, down), sems)
    slots = token_blocks[0].shape[0]
    partner = lax.axis_index("dp") ^ PARTNER
    copies[0].wait()
    column = row_to_column(weight[...])
    copies[1].wait()
    scaled = (column * out_grad[...].astype(F32)).astype(BF)
    sent = dot(placed[...], scaled, 1, 0).astype(BF)
    for k in range(experts):
        blocks[k][...] = sent[k * slots:(k + 1) * slots]
    for k, half in enumerate(blocks[experts:]):
        columns_for(token_blocks[k], half, partner, width)
        columns_for(blocks[k], half, partner, width, len(MASKS) * width)
    copies[2].wait()
    copies[3].wait()


def columns_for(rows, out, device, width, start=0):
    for k, mask in enumerate(MASKS):
        at = pl.multiple_of((device ^ mask) * width, width)
        out[:, start + k * width:start + (k + 1) * width] = rows[:, pl.ds(at, width)]


def gather(blocks, rows):
    slots = blocks[0].shape[0]
    for k, block in enumerate(blocks):
        rows[k * slots:(k + 1) * slots, :] = block[...]


def forward_body(experts, width, *refs):
    blocks, (gate_up, pre_out, own, send, rows) = refs[:experts], refs[experts:]
    gather(blocks, rows)
    pre = dot(rows[...], gate_up[0], 1, 0)
    pre_out[...] = pre
    hidden = pre.shape[1] // 2
    gate, up = pre[:, :hidden], pre[:, hidden:]
    send[:, :hidden] = (gate * jax.nn.sigmoid(gate) * up).astype(BF)
    if width == 0:
        return
    device = lax.axis_index("dp")
    columns_for(rows, own, device, width)
    late = rows.shape[0] // 2
    for k, mask in enumerate(MASKS):
        at = pl.multiple_of((device ^ PARTNER ^ mask) * width, width)
        to, start = (k // 2) * late, hidden + (k % 2) * width
        send[to:to + late, start:start + width] = rows[late:, pl.ds(at, width)]


def backward_body(experts, width, *refs):
    blocks, (pre, down, own, send, d_gate, d_up, rows) = refs[:experts], refs[experts:]
    gather(blocks, rows)
    d_act = dot(rows[...], down[0], 1, 1)
    hidden = d_act.shape[1]
    gate, up = pre[:, :hidden], pre[:, hidden:]
    sig = jax.nn.sigmoid(gate)
    d_gate[...] = (d_act * up * sig * (1.0 + gate * (1.0 - sig))).astype(BF)
    d_up[...] = (d_act * (gate * sig)).astype(BF)
    if width == 0:
        return
    device = lax.axis_index("dp")
    columns_for(rows, own, device, width)
    late = rows.shape[0] // 2
    columns_for(rows.at[late:], send, device ^ PARTNER, width)


def return_body(experts, first, d_gate, d_up, gate_up, down, *blocks):
    slots = blocks[0].shape[0] // 2
    result = dot(first[:, :down.shape[1]], down[0], 1, 0).astype(BF)
    for k in range(experts):
        blocks[k][:slots] = result[k * slots:(k + 1) * slots]
    hidden = d_gate.shape[1]
    moved = dot(d_gate[...], gate_up[0, :, :hidden], 1, 1)
    moved = (moved + dot(d_up[...], gate_up[0, :, hidden:], 1, 1)).astype(BF)
    for k in range(experts):
        blocks[k][slots:] = moved[k * slots:(k + 1) * slots]


def terms_body(joined, hidden, *refs):
    halves, (own, factor, factor_in, late, kept, far, near, rows) = refs[:joined], refs[joined:]
    width, half = kept.shape[0], own.shape[1]
    slots, cut = halves[0].shape[0], rows.shape[0] // 2
    start = 0 if hidden else half
    for k, block in enumerate(halves):
        rows[k * slots:(k + 1) * slots, :] = block[:, start:start + half]
    if hidden:
        rows[cut:, :half // 2] = late[:cut, hidden:]
        rows[cut:, half // 2:] = late[cut:, hidden:]
    else:
        rows[cut:, :] = late[...]
    columns = kept.shape[1]
    for k, out in enumerate((kept, near.at[:width], far, near.at[width:])):
        at = slice(k * width, (k + 1) * width)
        total = dot(own[:, at], factor[:, :columns], 0, 0) + dot(rows[:, at], factor_in[:, :columns], 0, 0)
        out[...] = total.astype(out.dtype)


def pair_body(far, arrived, out):
    out[...] = (far[...] + arrived[far.shape[0]:, :].astype(F32)).astype(BF)


def total_of(kept, near, distant):
    return kept[...] + near[:kept.shape[0], :].astype(F32) + distant[...].astype(F32)


def early_body(*refs):
    first, second, (out, held, sems) = refs[:3], refs[3:6], refs[6:]
    width = held.shape[2]
    copies = []
    for k, terms in enumerate((first, second)):
        held[k] = total_of(*terms)
        target = out.at[:, pl.ds(2 * k * width, width)]
        copies.append(pltpu.make_async_copy(held.at[k], target, sems.at[k]))
        copies[k].start()
    for copy in copies:
        copy.wait()


def last_body(kept, near, distant, out_in, out, held, sem):
    held[...] = total_of(kept, near, distant)
    width = held.shape[1]
    copy = pltpu.make_async_copy(held, out.at[:, pl.ds(width, width)], sem)
    copy.start()
    copy.wait()


def combine_body(experts, *refs):
    blocks = refs[:experts]
    placed, weight, out_grad, mixed, token_grad, weight_out, rows = refs[experts:]
    slots = blocks[0].shape[0] // 2
    for k in range(experts):
        rows[k * slots:(k + 1) * slots, :] = blocks[k][:slots]
    copy_out = dot(placed[...], rows[...], 0, 0)
    mixed[...] = (row_to_column(weight[...]) * copy_out).astype(BF)
    products = jnp.sum(out_grad[...].astype(F32) * copy_out, axis=1, keepdims=True)
    weight_out[...] = column_to_row(products)
    for k in range(experts):
        rows[k * slots:(k + 1) * slots, :] = blocks[k][slots:]
    token_grad[...] = dot(placed[...], rows[...], 0, 0).astype(BF)


def permute(array, axis, size, step):
    return lax.ppermute(array, axis, [(i, i ^ step) for i in range(size)])


def exchange(blocks, axis, size, stride=1):
    return [blocks[0]] + [permute(blocks[k], axis, size, k * stride) for k in range(1, len(blocks))]


def across(block, k, experts, shards):
    pairs = [
        (i * experts + j, (i ^ PARTNER) * experts + (j ^ k)) for i in range(shards) for j in range(experts)
    ]
    return lax.ppermute(block, ("dp", "expert"), pairs)


def on_device(tokens, route_ids, route_weight, w_gate_up, w_down, out_grad):
    experts, shards = lax.axis_size("expert"), lax.axis_size("dp")
    count, top = route_ids.shape
    assert top == 1
    width = tokens.shape[1]
    hidden = w_down.shape[1]
    capacity = 3 * count // (2 * experts)
    slots = -(-capacity // 16) * 16
    rows = experts * slots
    share = width // shards
    staged = is_staged(width, shards)
    half = len(MASKS) * share if staged else 256
    ids = route_ids.reshape(1, count)
    weight = route_weight.reshape(1, count)

    block = shape((slots, width), BF)
    placed, *sent_tokens = call(
        functools.partial(tokens_body, experts, slots),
        [shape((rows, count), BF)] + [block] * experts, (ids, tokens),
        [pltpu.VMEM(a.shape, a.dtype) for a in (ids, tokens)] + [pltpu.SemaphoreType.DMA((2,))],
        flops=2 * rows * count * width, far_ins=(0, 1))
    token_blocks = exchange(sent_tokens, "expert", experts)
    joined = experts // 2 if staged else 0
    gate_up, down, *sent = call(
        functools.partial(grads_body, experts, share),
        [shape(w_gate_up.shape, BF), shape(w_down.shape, BF)] + [block] * experts
        + [shape((slots, 2 * half), BF)] * joined,
        (placed, *sent_tokens, weight, out_grad, w_gate_up, w_down),
        [pltpu.VMEM(a.shape, a.dtype) for a in (weight, out_grad)] + [pltpu.SemaphoreType.DMA((4,))],
        flops=2 * rows * count * width, far_ins=tuple(range(experts + 1, experts + 5)))
    grad_blocks = exchange(sent[:experts], "expert", experts)
    scratch = [pltpu.VMEM((rows, width), BF)]
    own_shape, late_shape = shape((rows, half), BF), shape((rows // 2, half), BF)
    piece = share if staged else 0
    pre, own_rows, first = call(
        functools.partial(forward_body, experts, piece),
        [shape((rows, 2 * hidden), F32), own_shape, shape((rows, hidden + half // 2), BF)],
        (*token_blocks, gate_up), scratch, flops=4 * rows * hidden * width)
    own_grads, late_grads, d_gate, d_up = call(
        functools.partial(backward_body, experts, piece),
        [own_shape, late_shape] + [shape((rows, hidden), BF)] * 2,
        (*grad_blocks, pre, down), scratch, flops=2 * rows * hidden * width)
    back = call(
        functools.partial(return_body, experts), [shape((2 * slots, width), BF)] * experts,
        (first, d_gate, d_up, gate_up, down), flops=6 * rows * hidden * width)
    if staged:
        first_in = permute(first, "dp", shards, PARTNER)
        both = [across(sent[experts + k], k, experts, shards) for k in range(joined)]
        late_in = permute(late_grads, "dp", shards, PARTNER)
        d_gate_in = permute(d_gate, "dp", shards, PARTNER)
        d_up_in = permute(d_up, "dp", shards, PARTNER)
        one = shape((share, hidden), F32)

        def summed(start, own, factor, factor_in, late):
            kept, far, near = call(
                functools.partial(terms_body, joined, start),
                [one, one, shape((2 * share, hidden), BF)], (*both, own, factor, factor_in, late),
                [pltpu.VMEM((rows, half), BF)], flops=4 * rows * hidden * half)
            near = permute(near, "dp", shards, MASKS[1])
            distant, = call(pair_body, [shape((share, hidden), BF)], (far, near))
            return kept, near, permute(distant, "dp", shards, MASKS[2])

        downs = summed(0, own_grads, first, first_in, late_in)
        gates = summed(hidden, own_rows, d_gate, d_gate_in, first_in)
        ups = summed(hidden, own_rows, d_up, d_up_in, first_in)
        whole = shape((share, 3 * hidden), F32)
        weight_grad, = call(
            early_body, [whole], (*gates, *downs),
            [pltpu.VMEM((2, share, hidden), F32), pltpu.SemaphoreType.DMA((2,))], far_outs=(0,))
        weight_grad, = call(
            last_body, [whole], (*ups, weight_grad),
            [pltpu.VMEM((share, hidden), F32), pltpu.SemaphoreType.DMA],
            far_ins=(3,), far_outs=(0,), aliases={3: 0})
    else:
        weight_grad = lax.psum_scatter(
            jnp.concatenate([
                dot(jnp.concatenate(token_blocks, axis=0), jnp.concatenate([d_gate, d_up], axis=1), 0, 0),
                dot(jnp.concatenate(grad_blocks, axis=0), first[:, :hidden], 0, 0)], axis=1),
            "dp", scatter_dimension=0, tiled=True)
    returned = exchange(back, "expert", experts)
    mixed, token_grad, weight_row = call(
        functools.partial(combine_body, experts),
        [shape((count, width), BF), shape((count, width), BF), shape((1, count), F32)],
        (*returned, placed, weight, out_grad), scratch, flops=4 * rows * count * width)
    return (mixed, token_grad, weight_row.reshape(count, 1), weight_grad[None])


def is_staged(width, shards):
    return shards == 8 and (width // shards) % 128 == 0


PARTNER = 2
MASKS = (0, 1, 4, 5)


def solution(mesh):
    split = P(("dp", "expert"), None)
    whole = P("expert", None, None)

    return jax.shard_map(
        on_device,
        mesh=mesh,
        in_specs=(split, split, split, whole, whole, split),
        out_specs=(split, split, split, P("expert", "dp", None)),
        check_vma=False,
    )
```

```python
import functools

import jax
import jax.numpy as jnp
from jax import lax
from jax.experimental import pallas as pl
from jax.experimental.pallas import tpu as pltpu
from jax.sharding import PartitionSpec as P


BF = jnp.bfloat16
F32 = jnp.float32
VMEM = pl.BlockSpec(memory_space=pltpu.VMEM)
FAR = pl.BlockSpec(memory_space=pltpu.HBM)


def dot(left, right, left_axis, right_axis):
    return lax.dot_general(
        left, right, (((left_axis,), (right_axis,)), ((), ())), preferred_element_type=F32
    )


def call(body, outs, args, scratch=(), flops=0, far_ins=(), far_outs=(), aliases=None):
    size = sum(a.size * a.dtype.itemsize for a in args)
    size += sum(o.size * o.dtype.itemsize for o in outs)
    args = [pltpu.with_memory_space_constraint(a, pltpu.HBM) if k in far_ins else a for k, a in enumerate(args)]
    return pl.pallas_call(
        body,
        out_shape=list(outs),
        in_specs=[FAR if k in far_ins else VMEM for k in range(len(args))],
        out_specs=[FAR if k in far_outs else VMEM for k in range(len(outs))],
        scratch_shapes=list(scratch),
        input_output_aliases=aliases or {},
        cost_estimate=pl.CostEstimate(flops=flops, bytes_accessed=size, transcendentals=0),
        compiler_params=pltpu.CompilerParams(vmem_limit_bytes=24 << 20),
    )(*args)


def shape(dims, dtype):
    return jax.ShapeDtypeStruct(dims, dtype)


def row_to_column(row):
    count = row.shape[1]
    at = lax.broadcasted_iota(jnp.int32, (count, count), 0)
    to = lax.broadcasted_iota(jnp.int32, (count, count), 1)
    return jnp.sum(jnp.where(at == to, jnp.broadcast_to(row, (count, count)), 0.0), axis=1, keepdims=True)


def column_to_row(column):
    count = column.shape[0]
    at = lax.broadcasted_iota(jnp.int32, (count, count), 0)
    to = lax.broadcasted_iota(jnp.int32, (count, count), 1)
    return jnp.sum(jnp.where(at == to, jnp.broadcast_to(column, (count, count)), 0.0), axis=0, keepdims=True)


def one_hot(ids, experts, slots):
    me = lax.axis_index("expert")
    count = ids.shape[1]
    padded = max(8, experts)
    kinds = lax.broadcasted_iota(jnp.int32, (padded, count), 0)
    here = kinds == jnp.broadcast_to(ids, (padded, count))
    onehot = jnp.where(here, 1.0, 0.0)
    at = lax.broadcasted_iota(jnp.int32, (count, count), 0)
    to = lax.broadcasted_iota(jnp.int32, (count, count), 1)
    earlier = jnp.where(at < to, 1.0, 0.0).astype(BF)
    before = dot(onehot.astype(BF), earlier, 1, 0)
    position = jnp.sum(before * onehot, axis=0, keepdims=True).astype(jnp.int32)
    slot = (ids ^ me) * slots + position
    rows = experts * slots
    place = lax.broadcasted_iota(jnp.int32, (rows, count), 0)
    return jnp.where(place == jnp.broadcast_to(slot, (rows, count)), 1.0, 0.0).astype(BF)


def copy_in(sources, targets, sems):
    copies = [pltpu.make_async_copy(s, t, sems.at[k]) for k, (s, t) in enumerate(zip(sources, targets))]
    for copy in copies:
        copy.start()
    return copies


def tokens_body(experts, slots, ids_in, tokens_in, placed_out, *refs):
    blocks, (ids, tokens, sems) = refs[:experts], refs[experts:]
    copies = copy_in((ids_in, tokens_in), (ids, tokens), sems)
    copies[0].wait()
    placed = one_hot(ids[...], experts, slots)
    placed_out[...] = placed
    copies[1].wait()
    sent = dot(placed, tokens[...], 1, 0).astype(BF)
    for k in range(experts):
        blocks[k][...] = sent[k * slots:(k + 1) * slots]


def grads_body(experts, *refs):
    placed, sources, (gate_up, down, *blocks) = refs[0], refs[1:5], refs[5:-3]
    weight, out_grad, sems = refs[-3:]
    copies = copy_in(sources, (weight, out_grad, gate_up, down), sems)
    slots = blocks[0].shape[0]
    copies[0].wait()
    column = row_to_column(weight[...])
    copies[1].wait()
    scaled = (column * out_grad[...].astype(F32)).astype(BF)
    sent = dot(placed[...], scaled, 1, 0).astype(BF)
    for k in range(experts):
        blocks[k][...] = sent[k * slots:(k + 1) * slots]
    copies[2].wait()
    copies[3].wait()


def columns_for(rows, out, device, masks, width):
    for k, mask in enumerate(masks):
        at = pl.multiple_of((device ^ mask) * width, width)
        out[:, k * width:(k + 1) * width] = rows[:, pl.ds(at, width)]


def gather(blocks, rows):
    slots = blocks[0].shape[0]
    for k, block in enumerate(blocks):
        rows[k * slots:(k + 1) * slots, :] = block[...]


def pack_body(blocks, width, *refs):
    sent, rows = refs[blocks:]
    gather(refs[:blocks], rows)
    columns_for(rows, sent, lax.axis_index("dp") ^ UP_PARTNER, UP_MASKS, width)


def forward_body(experts, width, *refs):
    blocks, (gate_up, pre_out, act, own, send, rows) = refs[:experts], refs[experts:]
    gather(blocks, rows)
    pre = dot(rows[...], gate_up[0], 1, 0)
    pre_out[...] = pre
    hidden = pre.shape[1] // 2
    gate, up = pre[:, :hidden], pre[:, hidden:]
    act[...] = (gate * jax.nn.sigmoid(gate) * up).astype(BF)
    if width:
        device = lax.axis_index("dp")
        columns_for(rows, own, device, UP_MASKS, width)
        late = rows.at[rows.shape[0] - send.shape[0]:]
        columns_for(late, send, device ^ UP_PARTNER, UP_MASKS, width)


def backward_body(experts, width, *refs):
    blocks, (pre, down, own, send, d_gate, d_up, rows) = refs[:experts], refs[experts:]
    gather(blocks, rows)
    d_act = dot(rows[...], down[0], 1, 1)
    hidden = d_act.shape[1]
    gate, up = pre[:, :hidden], pre[:, hidden:]
    sig = jax.nn.sigmoid(gate)
    d_gate[...] = (d_act * up * sig * (1.0 + gate * (1.0 - sig))).astype(BF)
    d_up[...] = (d_act * (gate * sig)).astype(BF)
    if width:
        device = lax.axis_index("dp")
        columns_for(rows, own, device, DOWN_MASKS, width)
        columns_for(rows, send, device ^ DOWN_PARTNER, DOWN_MASKS, width)


def return_body(experts, act, d_gate, d_up, gate_up, down, *blocks):
    slots = blocks[0].shape[0] // 2
    result = dot(act[...], down[0], 1, 0).astype(BF)
    for k in range(experts):
        blocks[k][:slots] = result[k * slots:(k + 1) * slots]
    hidden = d_gate.shape[1]
    moved = dot(d_gate[...], gate_up[0, :, :hidden], 1, 1)
    moved = (moved + dot(d_up[...], gate_up[0, :, hidden:], 1, 1)).astype(BF)
    for k in range(experts):
        blocks[k][slots:] = moved[k * slots:(k + 1) * slots]


def terms_body(order, pieces, own, factor, *refs):
    parts, (factor_in, kept, far, near, rows) = refs[:pieces], refs[pieces:]
    start = 0
    for part in parts:
        rows[start:start + part.shape[0], :] = part[...]
        start += part.shape[0]
    width = kept.shape[0]
    for k, out in zip(order, (kept, near.at[:width], far, near.at[width:])):
        at = slice(k * width, (k + 1) * width)
        total = dot(own[:, at], factor[...], 0, 0) + dot(rows[:, at], factor_in[...], 0, 0)
        out[...] = total.astype(out.dtype)


def pair_body(far, arrived, out):
    out[...] = (far[...] + arrived[far.shape[0]:, :].astype(F32)).astype(BF)


def total_of(kept, near, distant):
    return kept[...] + near[:kept.shape[0], :].astype(F32) + distant[...].astype(F32)


def early_body(places, *refs):
    first, second, (out, held, sems) = refs[:3], refs[3:6], refs[6:]
    width = held.shape[2]
    copies = []
    for k, terms in enumerate((first, second)):
        held[k] = total_of(*terms)
        target = out.at[:, pl.ds(places[k] * width, width)]
        copies.append(pltpu.make_async_copy(held.at[k], target, sems.at[k]))
        copies[k].start()
    for copy in copies:
        copy.wait()


def last_body(place, kept, near, distant, out_in, out, held, sem):
    held[...] = total_of(kept, near, distant)
    width = held.shape[1]
    copy = pltpu.make_async_copy(held, out.at[:, pl.ds(place * width, width)], sem)
    copy.start()
    copy.wait()


def combine_body(experts, *refs):
    blocks = refs[:experts]
    placed, weight, out_grad, mixed, token_grad, weight_out, rows = refs[experts:]
    slots = blocks[0].shape[0] // 2
    for k in range(experts):
        rows[k * slots:(k + 1) * slots, :] = blocks[k][:slots]
    copy_out = dot(placed[...], rows[...], 0, 0)
    mixed[...] = (row_to_column(weight[...]) * copy_out).astype(BF)
    products = jnp.sum(out_grad[...].astype(F32) * copy_out, axis=1, keepdims=True)
    weight_out[...] = column_to_row(products)
    for k in range(experts):
        rows[k * slots:(k + 1) * slots, :] = blocks[k][slots:]
    token_grad[...] = dot(placed[...], rows[...], 0, 0).astype(BF)


def permute(array, axis, size, step):
    return lax.ppermute(array, axis, [(i, i ^ step) for i in range(size)])


def exchange(blocks, axis, size, stride=1):
    return [blocks[0]] + [permute(blocks[k], axis, size, k * stride) for k in range(1, len(blocks))]


def on_device(tokens, route_ids, route_weight, w_gate_up, w_down, out_grad):
    experts, shards = lax.axis_size("expert"), lax.axis_size("dp")
    count, top = route_ids.shape
    assert top == 1
    width = tokens.shape[1]
    hidden = w_down.shape[1]
    capacity = 3 * count // (2 * experts)
    slots = -(-capacity // 16) * 16
    rows = experts * slots
    share = width // shards
    staged = is_staged(width, shards)
    half = 4 * share if staged else 128
    ids = route_ids.reshape(1, count)
    weight = route_weight.reshape(1, count)

    block = shape((slots, width), BF)
    placed, *sent_tokens = call(
        functools.partial(tokens_body, experts, slots),
        [shape((rows, count), BF)] + [block] * experts, (ids, tokens),
        [pltpu.VMEM(a.shape, a.dtype) for a in (ids, tokens)] + [pltpu.SemaphoreType.DMA((2,))],
        flops=2 * rows * count * width, far_ins=(0, 1))
    token_blocks = exchange(sent_tokens, "expert", experts)
    gate_up, down, *sent = call(
        functools.partial(grads_body, experts),
        [shape(w_gate_up.shape, BF), shape(w_down.shape, BF)] + [block] * experts,
        (placed, weight, out_grad, w_gate_up, w_down),
        [pltpu.VMEM(a.shape, a.dtype) for a in (weight, out_grad)] + [pltpu.SemaphoreType.DMA((4,))],
        flops=2 * rows * count * width, far_ins=(1, 2, 3, 4))
    grad_blocks = exchange(sent[:experts], "expert", experts)
    scratch = [pltpu.VMEM((rows, width), BF)]
    side = shape((rows, half), BF)
    early = experts // 2
    part = shape((early * slots, half), BF)
    piece = share if staged else 0
    pre, act, own_rows, sent_rows = call(
        functools.partial(forward_body, experts, piece),
        [shape((rows, 2 * hidden), F32), shape((rows, hidden), BF), side, part],
        (*token_blocks, gate_up), scratch, flops=4 * rows * hidden * width)
    own_grads, late_grads, d_gate, d_up = call(
        functools.partial(backward_body, experts, piece),
        [side, side] + [shape((rows, hidden), BF)] * 2,
        (*grad_blocks, pre, down), scratch, flops=2 * rows * hidden * width)
    back = call(
        functools.partial(return_body, experts), [shape((2 * slots, width), BF)] * experts,
        (act, d_gate, d_up, gate_up, down), flops=6 * rows * hidden * width)
    if staged:
        act_in = permute(act, "dp", shards, DOWN_PARTNER)
        packed, = call(
            functools.partial(pack_body, early, share), [part], token_blocks[:early],
            [pltpu.VMEM((early * slots, width), BF)])
        rows_in = [permute(packed, "dp", shards, UP_PARTNER), permute(sent_rows, "dp", shards, UP_PARTNER)]
        grads_in = [permute(late_grads, "dp", shards, DOWN_PARTNER)]
        d_gate_in = permute(d_gate, "dp", shards, UP_PARTNER)
        d_up_in = permute(d_up, "dp", shards, UP_PARTNER)
        one = shape((share, hidden), F32)

        def summed(own, factor, rows_in, factor_in, masks, order):
            kept, far, near = call(
                functools.partial(terms_body, order, len(rows_in)),
                [one, one, shape((2 * share, hidden), BF)], (own, factor, *rows_in, factor_in),
                [pltpu.VMEM((rows, half), BF)], flops=4 * rows * hidden * half)
            near = permute(near, "dp", shards, masks[order[1]])
            distant, = call(pair_body, [shape((share, hidden), BF)], (far, near))
            return kept, near, permute(distant, "dp", shards, masks[order[2]])

        gates = summed(own_rows, d_gate, rows_in, d_gate_in, UP_MASKS, GATE_ORDER)
        downs = summed(own_grads, act, grads_in, act_in, DOWN_MASKS, DOWN_ORDER)
        ups = summed(own_rows, d_up, rows_in, d_up_in, UP_MASKS, UP_ORDER)
        whole = shape((share, 3 * hidden), F32)
        terms = [gates, ups, downs]
        first, second, final = FINISH
        weight_grad, = call(
            functools.partial(early_body, (first, second)), [whole],
            (*terms[first], *terms[second]),
            [pltpu.VMEM((2, share, hidden), F32), pltpu.SemaphoreType.DMA((2,))], far_outs=(0,))
        weight_grad, = call(
            functools.partial(last_body, final), [whole], (*terms[final], weight_grad),
            [pltpu.VMEM((share, hidden), F32), pltpu.SemaphoreType.DMA],
            far_ins=(3,), far_outs=(0,), aliases={3: 0})
    else:
        weight_grad = lax.psum_scatter(
            jnp.concatenate([
                dot(jnp.concatenate(token_blocks, axis=0), jnp.concatenate([d_gate, d_up], axis=1), 0, 0),
                dot(jnp.concatenate(grad_blocks, axis=0), act, 0, 0)], axis=1),
            "dp", scatter_dimension=0, tiled=True)
    returned = exchange(back, "expert", experts)
    mixed, token_grad, weight_row = call(
        functools.partial(combine_body, experts),
        [shape((count, width), BF), shape((count, width), BF), shape((1, count), F32)],
        (*returned, placed, weight, out_grad), scratch, flops=4 * rows * count * width)
    return (mixed, token_grad, weight_row.reshape(count, 1), weight_grad[None])


def is_staged(width, shards):
    return shards == 8 and (width // shards) % 128 == 0


DOWN_PARTNER, DOWN_MASKS = 1, (0, 2, 4, 6)
UP_PARTNER, UP_MASKS = 2, (0, 1, 4, 5)
FINISH = (0, 1, 2)
GATE_ORDER = (0, 2, 1, 3)
DOWN_ORDER = UP_ORDER = (0, 1, 2, 3)


def solution(mesh):
    split = P(("dp", "expert"), None)
    whole = P("expert", None, None)

    return jax.shard_map(
        on_device,
        mesh=mesh,
        in_specs=(split, split, split, whole, whole, split),
        out_specs=(split, split, split, P("expert", "dp", None)),
        check_vma=False,
    )
```

```python
import functools

import jax
import jax.numpy as jnp
from jax import lax
from jax.experimental import pallas as pl
from jax.experimental.pallas import tpu as pltpu
from jax.sharding import PartitionSpec as P


BF = jnp.bfloat16
F32 = jnp.float32
VMEM = pl.BlockSpec(memory_space=pltpu.VMEM)
FAR = pl.BlockSpec(memory_space=pltpu.HBM)


def dot(left, right, left_axis, right_axis):
    return lax.dot_general(
        left, right, (((left_axis,), (right_axis,)), ((), ())), preferred_element_type=F32
    )


def call(body, outs, args, scratch=(), flops=0, far_ins=(), far_outs=(), aliases=None):
    size = sum(a.size * a.dtype.itemsize for a in args)
    size += sum(o.size * o.dtype.itemsize for o in outs)
    args = [pltpu.with_memory_space_constraint(a, pltpu.HBM) if k in far_ins else a for k, a in enumerate(args)]
    return pl.pallas_call(
        body,
        out_shape=list(outs),
        in_specs=[FAR if k in far_ins else VMEM for k in range(len(args))],
        out_specs=[FAR if k in far_outs else VMEM for k in range(len(outs))],
        scratch_shapes=list(scratch),
        input_output_aliases=aliases or {},
        cost_estimate=pl.CostEstimate(flops=flops, bytes_accessed=size, transcendentals=0),
        compiler_params=pltpu.CompilerParams(vmem_limit_bytes=24 << 20),
    )(*args)


def shape(dims, dtype):
    return jax.ShapeDtypeStruct(dims, dtype)


def row_to_column(row):
    count = row.shape[1]
    at = lax.broadcasted_iota(jnp.int32, (count, count), 0)
    to = lax.broadcasted_iota(jnp.int32, (count, count), 1)
    return jnp.sum(jnp.where(at == to, jnp.broadcast_to(row, (count, count)), 0.0), axis=1, keepdims=True)


def column_to_row(column):
    count = column.shape[0]
    at = lax.broadcasted_iota(jnp.int32, (count, count), 0)
    to = lax.broadcasted_iota(jnp.int32, (count, count), 1)
    return jnp.sum(jnp.where(at == to, jnp.broadcast_to(column, (count, count)), 0.0), axis=0, keepdims=True)


def one_hot(ids, experts, slots):
    me = lax.axis_index("expert")
    count = ids.shape[1]
    padded = max(8, experts)
    kinds = lax.broadcasted_iota(jnp.int32, (padded, count), 0)
    here = kinds == jnp.broadcast_to(ids, (padded, count))
    onehot = jnp.where(here, 1.0, 0.0)
    at = lax.broadcasted_iota(jnp.int32, (count, count), 0)
    to = lax.broadcasted_iota(jnp.int32, (count, count), 1)
    earlier = jnp.where(at < to, 1.0, 0.0).astype(BF)
    before = dot(onehot.astype(BF), earlier, 1, 0)
    position = jnp.sum(before * onehot, axis=0, keepdims=True).astype(jnp.int32)
    slot = (ids ^ me) * slots + position
    rows = experts * slots
    place = lax.broadcasted_iota(jnp.int32, (rows, count), 0)
    return jnp.where(place == jnp.broadcast_to(slot, (rows, count)), 1.0, 0.0).astype(BF)


def copy_in(sources, targets, sems):
    copies = [pltpu.make_async_copy(s, t, sems.at[k]) for k, (s, t) in enumerate(zip(sources, targets))]
    for copy in copies:
        copy.start()
    return copies


def tokens_body(experts, slots, ids_in, tokens_in, placed_out, *refs):
    blocks, (ids, tokens, sems) = refs[:experts], refs[experts:]
    copies = copy_in((ids_in, tokens_in), (ids, tokens), sems)
    copies[0].wait()
    placed = one_hot(ids[...], experts, slots)
    placed_out[...] = placed
    copies[1].wait()
    sent = dot(placed, tokens[...], 1, 0).astype(BF)
    for k in range(experts):
        blocks[k][...] = sent[k * slots:(k + 1) * slots]


def grads_body(experts, *refs):
    placed, sources, (gate_up, down, *blocks) = refs[0], refs[1:5], refs[5:-3]
    weight, out_grad, sems = refs[-3:]
    copies = copy_in(sources, (weight, out_grad, gate_up, down), sems)
    slots = blocks[0].shape[0]
    copies[0].wait()
    column = row_to_column(weight[...])
    copies[1].wait()
    scaled = (column * out_grad[...].astype(F32)).astype(BF)
    sent = dot(placed[...], scaled, 1, 0).astype(BF)
    for k in range(experts):
        blocks[k][...] = sent[k * slots:(k + 1) * slots]
    copies[2].wait()
    copies[3].wait()


def columns_for(rows, out, device, masks, width):
    for k, mask in enumerate(masks):
        at = pl.multiple_of((device ^ mask) * width, width)
        out[:, k * width:(k + 1) * width] = rows[:, pl.ds(at, width)]


def gather(blocks, rows):
    slots = blocks[0].shape[0]
    for k, block in enumerate(blocks):
        rows[k * slots:(k + 1) * slots, :] = block[...]


def forward_body(experts, width, *refs):
    blocks, (gate_up, pre_out, act, own, send, rows) = refs[:experts], refs[experts:]
    gather(blocks, rows)
    pre = dot(rows[...], gate_up[0], 1, 0)
    pre_out[...] = pre
    hidden = pre.shape[1] // 2
    gate, up = pre[:, :hidden], pre[:, hidden:]
    act[...] = (gate * jax.nn.sigmoid(gate) * up).astype(BF)
    if width:
        device = lax.axis_index("dp")
        columns_for(rows, own, device, UP_MASKS, width)
        columns_for(rows, send, device ^ UP_PARTNER, UP_MASKS, width)


def backward_body(experts, width, *refs):
    blocks, (pre, down, own, send, d_first, d_gate, d_up, rows) = refs[:experts], refs[experts:]
    gather(blocks, rows)
    d_act = dot(rows[...], down[0], 1, 1)
    hidden = d_act.shape[1]
    gate, up = pre[:, :hidden], pre[:, hidden:]
    sig = jax.nn.sigmoid(gate)
    both = (d_act * up * sig * (1.0 + gate * (1.0 - sig))).astype(BF)
    d_first[...] = both[:, :FIRST]
    d_gate[...] = both[:, FIRST:]
    d_up[...] = (d_act * (gate * sig)).astype(BF)
    if width:
        device = lax.axis_index("dp")
        columns_for(rows, own, device, DOWN_MASKS, width)
        columns_for(rows, send, device ^ DOWN_PARTNER, DOWN_MASKS, width)


def return_body(experts, act, d_first, d_gate, d_up, gate_up, down, *blocks):
    slots = blocks[0].shape[0] // 2
    result = dot(act[...], down[0], 1, 0).astype(BF)
    for k in range(experts):
        blocks[k][:slots] = result[k * slots:(k + 1) * slots]
    hidden = d_up.shape[1]
    moved = dot(d_first[...], gate_up[0, :, :FIRST], 1, 1)
    moved += dot(d_gate[...], gate_up[0, :, FIRST:hidden], 1, 1)
    moved = (moved + dot(d_up[...], gate_up[0, :, hidden:], 1, 1)).astype(BF)
    for k in range(experts):
        blocks[k][slots:] = moved[k * slots:(k + 1) * slots]


def terms_body(order, own, factor, rows_in, factor_in, kept, far, near):
    width = kept.shape[0]
    for k, out in zip(order, (kept, near.at[:width], far, near.at[width:])):
        at = slice(k * width, (k + 1) * width)
        total = dot(own[:, at], factor[...], 0, 0) + dot(rows_in[:, at], factor_in[...], 0, 0)
        out[...] = total.astype(out.dtype)


def pair_body(*refs):
    *terms, out = refs
    start = 0
    for far, arrived in zip(terms[::2], terms[1::2]):
        stop = start + far.shape[1]
        out[:, start:stop] = (far[...] + arrived[far.shape[0]:, :].astype(F32)).astype(BF)
        start = stop


def total_of(kept, near, distant):
    return kept[...] + near[:kept.shape[0], :].astype(F32) + distant[...].astype(F32)


def early_body(kept_a, near_a, kept_b, near_b, distant, *refs):
    (*ups, out, held, sem) = refs
    cut, hidden = kept_a.shape[1], distant.shape[1]
    held[:, :cut] = total_of(kept_a, near_a, distant.at[:, :cut])
    held[:, cut:hidden] = total_of(kept_b, near_b, distant.at[:, cut:])
    held[:, hidden:] = total_of(*ups)
    copy = pltpu.make_async_copy(held, out.at[:, pl.ds(0, held.shape[1])], sem)
    copy.start()
    copy.wait()


def last_body(kept, near, distant, out_in, out, held, sem):
    held[...] = total_of(kept, near, distant)
    width = held.shape[1]
    copy = pltpu.make_async_copy(held, out.at[:, pl.ds(out.shape[1] - width, width)], sem)
    copy.start()
    copy.wait()


def combine_body(experts, *refs):
    blocks = refs[:experts]
    placed, weight, out_grad, mixed, token_grad, weight_out, rows = refs[experts:]
    slots = blocks[0].shape[0] // 2
    for k in range(experts):
        rows[k * slots:(k + 1) * slots, :] = blocks[k][:slots]
    copy_out = dot(placed[...], rows[...], 0, 0)
    mixed[...] = (row_to_column(weight[...]) * copy_out).astype(BF)
    products = jnp.sum(out_grad[...].astype(F32) * copy_out, axis=1, keepdims=True)
    weight_out[...] = column_to_row(products)
    for k in range(experts):
        rows[k * slots:(k + 1) * slots, :] = blocks[k][slots:]
    token_grad[...] = dot(placed[...], rows[...], 0, 0).astype(BF)


def permute(array, axis, size, step):
    return lax.ppermute(array, axis, [(i, i ^ step) for i in range(size)])


def exchange(blocks, axis, size, stride=1):
    return [blocks[0]] + [permute(blocks[k], axis, size, k * stride) for k in range(1, len(blocks))]


def on_device(tokens, route_ids, route_weight, w_gate_up, w_down, out_grad):
    experts, shards = lax.axis_size("expert"), lax.axis_size("dp")
    count, top = route_ids.shape
    assert top == 1
    width = tokens.shape[1]
    hidden = w_down.shape[1]
    capacity = 3 * count // (2 * experts)
    slots = -(-capacity // 16) * 16
    rows = experts * slots
    share = width // shards
    staged = is_staged(width, shards)
    half = 4 * share if staged else 128
    ids = route_ids.reshape(1, count)
    weight = route_weight.reshape(1, count)

    block = shape((slots, width), BF)
    placed, *sent_tokens = call(
        functools.partial(tokens_body, experts, slots),
        [shape((rows, count), BF)] + [block] * experts, (ids, tokens),
        [pltpu.VMEM(a.shape, a.dtype) for a in (ids, tokens)] + [pltpu.SemaphoreType.DMA((2,))],
        flops=2 * rows * count * width, far_ins=(0, 1))
    token_blocks = exchange(sent_tokens, "expert", experts)
    gate_up, down, *sent = call(
        functools.partial(grads_body, experts),
        [shape(w_gate_up.shape, BF), shape(w_down.shape, BF)] + [block] * experts,
        (placed, weight, out_grad, w_gate_up, w_down),
        [pltpu.VMEM(a.shape, a.dtype) for a in (weight, out_grad)] + [pltpu.SemaphoreType.DMA((4,))],
        flops=2 * rows * count * width, far_ins=(1, 2, 3, 4))
    grad_blocks = exchange(sent[:experts], "expert", experts)
    scratch = [pltpu.VMEM((rows, width), BF)]
    side = shape((rows, half), BF)
    piece = share if staged else 0
    pre, act, own_rows, sent_rows = call(
        functools.partial(forward_body, experts, piece),
        [shape((rows, 2 * hidden), F32), shape((rows, hidden), BF), side, side],
        (*token_blocks, gate_up), scratch, flops=4 * rows * hidden * width)
    own_grads, sent_grads, d_first, d_gate, d_up = call(
        functools.partial(backward_body, experts, piece),
        [side, side] + [shape((rows, k), BF) for k in (FIRST, hidden - FIRST, hidden)],
        (*grad_blocks, pre, down), scratch, flops=2 * rows * hidden * width)
    back = call(
        functools.partial(return_body, experts), [shape((2 * slots, width), BF)] * experts,
        (act, d_first, d_gate, d_up, gate_up, down), flops=6 * rows * hidden * width)
    if staged:
        rows_in = permute(sent_rows, "dp", shards, UP_PARTNER)
        d_gate_in = permute(d_gate, "dp", shards, UP_PARTNER)
        d_up_in = permute(d_up, "dp", shards, UP_PARTNER)
        act_in = permute(act, "dp", shards, DOWN_PARTNER)
        grads_in = permute(sent_grads, "dp", shards, DOWN_PARTNER)

        def outs(columns):
            return [shape((share, columns), F32)] * 2 + [shape((2 * share, columns), BF)]

        def started(args, masks, order):
            columns = args[1].shape[1]
            kept, far, near = call(
                functools.partial(terms_body, order), outs(columns), args,
                flops=4 * rows * columns * half)
            return kept, far, permute(near, "dp", shards, masks[order[1]])

        def paired(terms, masks, order):
            columns = sum(far.shape[1] for far in terms[::2])
            distant, = call(pair_body, [shape((share, columns), BF)], terms)
            return permute(distant, "dp", shards, masks[order[2]])

        d_first_in = permute(d_first, "dp", shards, UP_PARTNER)
        kept_a, far_a, near_a = started((own_rows, d_first, rows_in, d_first_in), UP_MASKS, GATE_ORDER)
        kept_b, far_b, near_b = started((own_rows, d_gate, rows_in, d_gate_in), UP_MASKS, GATE_ORDER)
        distant = paired((far_a, near_a, far_b, near_b), UP_MASKS, GATE_ORDER)
        gates = (kept_a, near_a, kept_b, near_b, distant)
        kept, far, near = started((own_rows, d_up, rows_in, d_up_in), UP_MASKS, UP_ORDER)
        ups = (kept, near, paired((far, near), UP_MASKS, UP_ORDER))
        kept, far, near = started((own_grads, act, grads_in, act_in), DOWN_MASKS, DOWN_ORDER)
        downs = (kept, near, paired((far, near), DOWN_MASKS, DOWN_ORDER))
        whole = shape((share, 3 * hidden), F32)
        weight_grad, = call(
            early_body, [whole], (*gates, *ups),
            [pltpu.VMEM((share, 2 * hidden), F32), pltpu.SemaphoreType.DMA], far_outs=(0,))
        weight_grad, = call(
            last_body, [whole], (*downs, weight_grad),
            [pltpu.VMEM((share, hidden), F32), pltpu.SemaphoreType.DMA],
            far_ins=(3,), far_outs=(0,), aliases={3: 0})
    else:
        weight_grad = lax.psum_scatter(
            jnp.concatenate([
                dot(jnp.concatenate(token_blocks, axis=0), jnp.concatenate([d_first, d_gate, d_up], axis=1), 0, 0),
                dot(jnp.concatenate(grad_blocks, axis=0), act, 0, 0)], axis=1),
            "dp", scatter_dimension=0, tiled=True)
    returned = exchange(back, "expert", experts)
    mixed, token_grad, weight_row = call(
        functools.partial(combine_body, experts),
        [shape((count, width), BF), shape((count, width), BF), shape((1, count), F32)],
        (*returned, placed, weight, out_grad), scratch, flops=4 * rows * count * width)
    return (mixed, token_grad, weight_row.reshape(count, 1), weight_grad[None])


def is_staged(width, shards):
    return shards == 8 and (width // shards) % 128 == 0


DOWN_PARTNER, DOWN_MASKS = 1, (0, 2, 4, 6)
UP_PARTNER, UP_MASKS = 2, (0, 1, 4, 5)
FIRST = 128
GATE_ORDER = (0, 2, 1, 3)
DOWN_ORDER = (0, 1, 2, 3)
UP_ORDER = (0, 1, 2, 3)


def solution(mesh):
    split = P(("dp", "expert"), None)
    whole = P("expert", None, None)

    return jax.shard_map(
        on_device,
        mesh=mesh,
        in_specs=(split, split, split, whole, whole, split),
        out_specs=(split, split, split, P("expert", "dp", None)),
        check_vma=False,
    )
```

```python
import functools

import jax
import jax.numpy as jnp
from jax import lax
from jax.experimental import pallas as pl
from jax.experimental.pallas import tpu as pltpu
from jax.sharding import PartitionSpec as P


BF = jnp.bfloat16
F32 = jnp.float32
VMEM = pl.BlockSpec(memory_space=pltpu.VMEM)
FAR = pl.BlockSpec(memory_space=pltpu.HBM)


def dot(left, right, left_axis, right_axis):
    return lax.dot_general(
        left, right, (((left_axis,), (right_axis,)), ((), ())), preferred_element_type=F32
    )


def call(body, outs, args, scratch=(), flops=0, far_ins=(), far_outs=(), aliases=None):
    size = sum(a.size * a.dtype.itemsize for a in args)
    size += sum(o.size * o.dtype.itemsize for o in outs)
    args = [pltpu.with_memory_space_constraint(a, pltpu.HBM) if k in far_ins else a for k, a in enumerate(args)]
    return pl.pallas_call(
        body,
        out_shape=list(outs),
        in_specs=[FAR if k in far_ins else VMEM for k in range(len(args))],
        out_specs=[FAR if k in far_outs else VMEM for k in range(len(outs))],
        scratch_shapes=list(scratch),
        input_output_aliases=aliases or {},
        cost_estimate=pl.CostEstimate(flops=flops, bytes_accessed=size, transcendentals=0),
        compiler_params=pltpu.CompilerParams(vmem_limit_bytes=24 << 20),
    )(*args)


def shape(dims, dtype):
    return jax.ShapeDtypeStruct(dims, dtype)


def row_to_column(row):
    count = row.shape[1]
    at = lax.broadcasted_iota(jnp.int32, (count, count), 0)
    to = lax.broadcasted_iota(jnp.int32, (count, count), 1)
    return jnp.sum(jnp.where(at == to, jnp.broadcast_to(row, (count, count)), 0.0), axis=1, keepdims=True)


def column_to_row(column):
    count = column.shape[0]
    at = lax.broadcasted_iota(jnp.int32, (count, count), 0)
    to = lax.broadcasted_iota(jnp.int32, (count, count), 1)
    return jnp.sum(jnp.where(at == to, jnp.broadcast_to(column, (count, count)), 0.0), axis=0, keepdims=True)


def one_hot(ids, earlier, experts, slots):
    me = lax.axis_index("expert")
    count = ids.shape[1]
    padded = max(8, experts)
    kinds = lax.broadcasted_iota(jnp.int32, (padded, count), 0)
    here = kinds == jnp.broadcast_to(ids, (padded, count))
    onehot = jnp.where(here, 1.0, 0.0)
    before = dot(onehot.astype(BF), earlier, 1, 0)
    position = jnp.sum(before * onehot, axis=0, keepdims=True).astype(jnp.int32)
    slot = (ids ^ me) * slots + position
    rows = experts * slots
    place = lax.broadcasted_iota(jnp.int32, (rows, count), 0)
    return jnp.where(place == jnp.broadcast_to(slot, (rows, count)), 1.0, 0.0).astype(BF)


def copy_in(sources, targets, sems):
    copies = [pltpu.make_async_copy(s, t, sems.at[k]) for k, (s, t) in enumerate(zip(sources, targets))]
    for copy in copies:
        copy.start()
    return copies


def tokens_body(experts, slots, ids_in, tokens_in, placed_out, *refs):
    blocks, (ids, tokens, sems) = refs[:experts], refs[experts:]
    copies = copy_in((ids_in, tokens_in), (ids, tokens), sems)
    count = ids.shape[1]
    at = lax.broadcasted_iota(jnp.int32, (count, count), 0)
    to = lax.broadcasted_iota(jnp.int32, (count, count), 1)
    earlier = jnp.where(at < to, 1.0, 0.0).astype(BF)
    copies[0].wait()
    placed = one_hot(ids[...], earlier, experts, slots)
    placed_out[...] = placed
    copies[1].wait()
    sent = dot(placed, tokens[...], 1, 0).astype(BF)
    for k in range(experts):
        blocks[k][...] = sent[k * slots:(k + 1) * slots]


def grads_body(experts, *refs):
    placed, sources, (gate_up, down, *blocks) = refs[0], refs[1:5], refs[5:-3]
    weight, out_grad, sems = refs[-3:]
    copies = copy_in(sources, (weight, out_grad, gate_up, down), sems)
    slots = blocks[0].shape[0]
    copies[0].wait()
    column = row_to_column(weight[...])
    copies[1].wait()
    scaled = (column * out_grad[...].astype(F32)).astype(BF)
    sent = dot(placed[...], scaled, 1, 0).astype(BF)
    for k in range(experts):
        blocks[k][...] = sent[k * slots:(k + 1) * slots]
    copies[2].wait()
    copies[3].wait()


def columns_for(rows, out, device, masks, width):
    for k, mask in enumerate(masks):
        at = pl.multiple_of((device ^ mask) * width, width)
        out[:, k * width:(k + 1) * width] = rows[:, pl.ds(at, width)]


def gather(blocks, rows):
    slots = blocks[0].shape[0]
    for k, block in enumerate(blocks):
        rows[k * slots:(k + 1) * slots, :] = block[...]


def forward_body(experts, width, *refs):
    blocks, (gate_up, pre_out, act, own, send, rows) = refs[:experts], refs[experts:]
    gather(blocks, rows)
    pre = dot(rows[...], gate_up[0], 1, 0)
    pre_out[...] = pre
    hidden = pre.shape[1] // 2
    gate, up = pre[:, :hidden], pre[:, hidden:]
    act[...] = (gate * jax.nn.sigmoid(gate) * up).astype(BF)
    if width:
        device = lax.axis_index("dp")
        columns_for(rows, own, device, UP_MASKS, width)
        columns_for(rows, send, device ^ UP_PARTNER, UP_MASKS, width)


def backward_body(experts, width, *refs):
    blocks, (pre, down, own, send, d_first, d_gate, d_up, rows) = refs[:experts], refs[experts:]
    gather(blocks, rows)
    d_act = dot(rows[...], down[0], 1, 1)
    hidden = d_act.shape[1]
    gate, up = pre[:, :hidden], pre[:, hidden:]
    sig = jax.nn.sigmoid(gate)
    both = (d_act * up * sig * (1.0 + gate * (1.0 - sig))).astype(BF)
    d_first[...] = both[:, :FIRST]
    d_gate[...] = both[:, FIRST:]
    d_up[...] = (d_act * (gate * sig)).astype(BF)
    if width:
        device = lax.axis_index("dp")
        columns_for(rows, own, device, DOWN_MASKS, width)
        columns_for(rows, send, device ^ DOWN_PARTNER, DOWN_MASKS, width)


def return_body(experts, act, d_first, d_gate, d_up, gate_up, down, *blocks):
    slots = blocks[0].shape[0] // 2
    result = dot(act[...], down[0], 1, 0).astype(BF)
    for k in range(experts):
        blocks[k][:slots] = result[k * slots:(k + 1) * slots]
    hidden = d_up.shape[1]
    moved = dot(d_first[...], gate_up[0, :, :FIRST], 1, 1)
    moved += dot(d_gate[...], gate_up[0, :, FIRST:hidden], 1, 1)
    moved = (moved + dot(d_up[...], gate_up[0, :, hidden:], 1, 1)).astype(BF)
    for k in range(experts):
        blocks[k][slots:] = moved[k * slots:(k + 1) * slots]


def terms_body(order, own, factor, rows_in, factor_in, kept, far, near):
    width = kept.shape[0]
    for k, out in zip(order, (kept, near.at[:width], far, near.at[width:])):
        at = slice(k * width, (k + 1) * width)
        total = dot(own[:, at], factor[...], 0, 0) + dot(rows_in[:, at], factor_in[...], 0, 0)
        out[...] = total.astype(out.dtype)


def pair_body(*refs):
    *terms, out = refs
    start = 0
    for far, arrived in zip(terms[::2], terms[1::2]):
        stop = start + far.shape[1]
        out[:, start:stop] = (far[...] + arrived[far.shape[0]:, :].astype(F32)).astype(BF)
        start = stop


def total_of(kept, near, distant):
    return kept[...] + near[:kept.shape[0], :].astype(F32) + distant[...].astype(F32)


def early_body(kept_a, near_a, kept_b, near_b, distant, *refs):
    (*ups, out, held, sem) = refs
    cut, hidden = kept_a.shape[1], distant.shape[1]
    held[:, :cut] = total_of(kept_a, near_a, distant.at[:, :cut])
    held[:, cut:hidden] = total_of(kept_b, near_b, distant.at[:, cut:])
    held[:, hidden:] = total_of(*ups)
    copy = pltpu.make_async_copy(held, out.at[:, pl.ds(0, held.shape[1])], sem)
    copy.start()
    copy.wait()


def last_body(kept, near, distant, out_in, out, held, sems):
    count, width = held.shape
    copies = []
    for k in range(2):
        part = slice(k * count // 2, (k + 1) * count // 2)
        held[part] = kept[part] + near[part].astype(F32) + distant[part].astype(F32)
        target = out.at[part, pl.ds(out.shape[1] - width, width)]
        copies.append(pltpu.make_async_copy(held.at[part], target, sems.at[k]))
        copies[k].start()
    for copy in copies:
        copy.wait()


def combine_body(experts, *refs):
    blocks = refs[:experts]
    placed, weight, out_grad, mixed, token_grad, weight_out, rows = refs[experts:]
    slots = blocks[0].shape[0] // 2
    for k in range(experts):
        rows[k * slots:(k + 1) * slots, :] = blocks[k][:slots]
    copy_out = dot(placed[...], rows[...], 0, 0)
    mixed[...] = (row_to_column(weight[...]) * copy_out).astype(BF)
    products = jnp.sum(out_grad[...].astype(F32) * copy_out, axis=1, keepdims=True)
    weight_out[...] = column_to_row(products)
    for k in range(experts):
        rows[k * slots:(k + 1) * slots, :] = blocks[k][slots:]
    token_grad[...] = dot(placed[...], rows[...], 0, 0).astype(BF)


def permute(array, axis, size, step):
    return lax.ppermute(array, axis, [(i, i ^ step) for i in range(size)])


def exchange(blocks, axis, size, stride=1):
    return [blocks[0]] + [permute(blocks[k], axis, size, k * stride) for k in range(1, len(blocks))]


def on_device(tokens, route_ids, route_weight, w_gate_up, w_down, out_grad):
    experts, shards = lax.axis_size("expert"), lax.axis_size("dp")
    count, top = route_ids.shape
    assert top == 1
    width = tokens.shape[1]
    hidden = w_down.shape[1]
    capacity = 3 * count // (2 * experts)
    slots = -(-capacity // 16) * 16
    rows = experts * slots
    share = width // shards
    staged = is_staged(width, shards)
    half = 4 * share if staged else 128
    ids = route_ids.reshape(1, count)
    weight = route_weight.reshape(1, count)

    block = shape((slots, width), BF)
    placed, *sent_tokens = call(
        functools.partial(tokens_body, experts, slots),
        [shape((rows, count), BF)] + [block] * experts, (ids, tokens),
        [pltpu.VMEM(a.shape, a.dtype) for a in (ids, tokens)] + [pltpu.SemaphoreType.DMA((2,))],
        flops=2 * rows * count * width, far_ins=(0, 1))
    token_blocks = exchange(sent_tokens, "expert", experts)
    gate_up, down, *sent = call(
        functools.partial(grads_body, experts),
        [shape(w_gate_up.shape, BF), shape(w_down.shape, BF)] + [block] * experts,
        (placed, weight, out_grad, w_gate_up, w_down),
        [pltpu.VMEM(a.shape, a.dtype) for a in (weight, out_grad)] + [pltpu.SemaphoreType.DMA((4,))],
        flops=2 * rows * count * width, far_ins=(1, 2, 3, 4))
    grad_blocks = exchange(sent[:experts], "expert", experts)
    scratch = [pltpu.VMEM((rows, width), BF)]
    side = shape((rows, half), BF)
    piece = share if staged else 0
    pre, act, own_rows, sent_rows = call(
        functools.partial(forward_body, experts, piece),
        [shape((rows, 2 * hidden), F32), shape((rows, hidden), BF), side, side],
        (*token_blocks, gate_up), scratch, flops=4 * rows * hidden * width)
    own_grads, sent_grads, d_first, d_gate, d_up = call(
        functools.partial(backward_body, experts, piece),
        [side, side] + [shape((rows, k), BF) for k in (FIRST, hidden - FIRST, hidden)],
        (*grad_blocks, pre, down), scratch, flops=2 * rows * hidden * width)
    back = call(
        functools.partial(return_body, experts), [shape((2 * slots, width), BF)] * experts,
        (act, d_first, d_gate, d_up, gate_up, down), flops=6 * rows * hidden * width)
    if staged:
        rows_in = permute(sent_rows, "dp", shards, UP_PARTNER)
        d_gate_in = permute(d_gate, "dp", shards, UP_PARTNER)
        d_up_in = permute(d_up, "dp", shards, UP_PARTNER)
        act_in = permute(act, "dp", shards, DOWN_PARTNER)
        grads_in = permute(sent_grads, "dp", shards, DOWN_PARTNER)

        def outs(columns):
            return [shape((share, columns), F32)] * 2 + [shape((2 * share, columns), BF)]

        def started(args, masks, order):
            columns = args[1].shape[1]
            kept, far, near = call(
                functools.partial(terms_body, order), outs(columns), args,
                flops=4 * rows * columns * half)
            return kept, far, permute(near, "dp", shards, masks[order[1]])

        def paired(terms, masks, order):
            columns = sum(far.shape[1] for far in terms[::2])
            distant, = call(pair_body, [shape((share, columns), BF)], terms)
            return permute(distant, "dp", shards, masks[order[2]])

        d_first_in = permute(d_first, "dp", shards, UP_PARTNER)
        kept_a, far_a, near_a = started((own_rows, d_first, rows_in, d_first_in), UP_MASKS, GATE_ORDER)
        kept_b, far_b, near_b = started((own_rows, d_gate, rows_in, d_gate_in), UP_MASKS, GATE_ORDER)
        distant = paired((far_a, near_a, far_b, near_b), UP_MASKS, GATE_ORDER)
        gates = (kept_a, near_a, kept_b, near_b, distant)
        kept, far, near = started((own_rows, d_up, rows_in, d_up_in), UP_MASKS, UP_ORDER)
        ups = (kept, near, paired((far, near), UP_MASKS, UP_ORDER))
        kept, far, near = started((own_grads, act, grads_in, act_in), DOWN_MASKS, DOWN_ORDER)
        downs = (kept, near, paired((far, near), DOWN_MASKS, DOWN_ORDER))
        whole = shape((share, 3 * hidden), F32)
        weight_grad, = call(
            early_body, [whole], (*gates, *ups),
            [pltpu.VMEM((share, 2 * hidden), F32), pltpu.SemaphoreType.DMA], far_outs=(0,))
        weight_grad, = call(
            last_body, [whole], (*downs, weight_grad),
            [pltpu.VMEM((share, hidden), F32), pltpu.SemaphoreType.DMA((2,))],
            far_ins=(3,), far_outs=(0,), aliases={3: 0})
    else:
        weight_grad = lax.psum_scatter(
            jnp.concatenate([
                dot(jnp.concatenate(token_blocks, axis=0), jnp.concatenate([d_first, d_gate, d_up], axis=1), 0, 0),
                dot(jnp.concatenate(grad_blocks, axis=0), act, 0, 0)], axis=1),
            "dp", scatter_dimension=0, tiled=True)
    returned = exchange(back, "expert", experts)
    mixed, token_grad, weight_row = call(
        functools.partial(combine_body, experts),
        [shape((count, width), BF), shape((count, width), BF), shape((1, count), F32)],
        (*returned, placed, weight, out_grad), scratch, flops=4 * rows * count * width)
    return (mixed, token_grad, weight_row.reshape(count, 1), weight_grad[None])


def is_staged(width, shards):
    return shards == 8 and (width // shards) % 128 == 0


DOWN_PARTNER, DOWN_MASKS = 1, (0, 2, 4, 6)
UP_PARTNER, UP_MASKS = 2, (0, 1, 4, 5)
FIRST = 128
GATE_ORDER = (0, 2, 1, 3)
DOWN_ORDER = (0, 1, 2, 3)
UP_ORDER = (0, 1, 2, 3)


def solution(mesh):
    split = P(("dp", "expert"), None)
    whole = P("expert", None, None)

    return jax.shard_map(
        on_device,
        mesh=mesh,
        in_specs=(split, split, split, whole, whole, split),
        out_specs=(split, split, split, P("expert", "dp", None)),
        check_vma=False,
    )
```
